32 devices in a mesh: rows: 4 (over z), cols: 8 (over y, x, core).
Axes of the slice: x: 2, y: 2, z: 4, core: 2. Of those that a mesh axis runs over, the one named last changes fastest.
Arguments:
- right_side: float32 [256, 128, 256], P('rows', 'cols'), may hold values from -3 to 15
- initial: float32 [256, 128, 256], P('rows', 'cols'), may hold values from -0.15 to 2.15
- conduct: float32 [256, 128, 256], P('rows', 'cols'), may hold values from 0.5 to 2
Outputs:
- basis: float32 [5, 256, 128, 256], P(None, 'rows', 'cols')
- rfactor: float32 [5, 5], replicated
- updated: float32 [256, 128, 256], P('rows', 'cols')
The draws below stay inside these ranges and needn't reach their ends.
All inputs are finite; a program needn't handle non-finite values.
Results may differ from the reference program's by a relative error of at most 0.0028.
Values sent between devices are 32-bit elements; how exact they have to be, the bound alone decides.
A program may use at most 128 MiB of HBM per device.

```python
import math
import jax
import jax.numpy as jnp
import numpy as np
from jax import lax

CZ = 256
NX = 256
NY = 128


def smooth_profile():
    pos_x = (jnp.arange(NX, dtype=jnp.float32) + 0.5) / NX
    pos_y = (jnp.arange(NY, dtype=jnp.float32) + 0.5) / NY
    pos_z = (jnp.arange(CZ, dtype=jnp.float32) + 0.5) / CZ
    return jnp.sin(jnp.pi * pos_x)[:, None, None] * jnp.sin(jnp.pi * pos_y)[None, :, None] * jnp.sin(jnp.pi * pos_z)[None, None, :]


def draw_right_side(key, part):
    own_key = jax.random.fold_in(key, 11)
    height_key = jax.random.fold_in(own_key, 0)
    second_key = jax.random.fold_in(own_key, 2)
    height = jax.random.uniform(height_key, (), jnp.float32, 9.0, 12.0)
    pos_x = jnp.arange(NX, dtype=jnp.float32) / NX
    pos_y = jnp.arange(NY, dtype=jnp.float32) / NY
    amplitude = 10.0 ** (0.5 * (pos_x[:, None, None] + pos_y[None, :, None]) - 0.5)
    rough_part = 0.2 * jnp.clip(jax.random.normal(second_key, (NX, NY, CZ), jnp.float32), -4.0, 4.0)
    values = height * smooth_profile() + rough_part * amplitude
    return values.astype(jnp.float32)


def draw_initial(key, part):
    own_key = jax.random.fold_in(key, 23)
    height_key = jax.random.fold_in(own_key, 0)
    second_key = jax.random.fold_in(own_key, 2)
    height = jax.random.uniform(height_key, (), jnp.float32, 1.0, 2.0)
    rough_part = 0.035 * jnp.clip(jax.random.normal(second_key, (NX, NY, CZ), jnp.float32), -4.0, 4.0)
    values = height * smooth_profile() + rough_part
    return values.astype(jnp.float32)


def block_levels(key, dims, cuts, smallest, high):
    loudness = 1.0
    for position, parts in cuts:
        steps = jax.random.uniform(jax.random.fold_in(jax.random.fold_in(key, 6), position), (parts,), jnp.float32, smallest / len(cuts), high / len(cuts))
        loudness = loudness * jnp.repeat(jnp.exp(steps), dims[position] // parts).reshape((-1,) + (1,) * (len(dims) - 1 - position))
    return loudness


def setup_inputs(seed: int = 0) -> dict:
    key_list = jax.random.split(jax.random.key(seed), 4)
    return {
        "right_side": draw_right_side(jax.random.fold_in(key_list[3], 71), 0),
        "initial": draw_initial(jax.random.fold_in(key_list[3], 71), 0),
        "conduct": jnp.clip(jnp.exp(math.log(2.0) - 1.3862944 * jax.random.uniform(key_list[2], (NX, NY, CZ), jnp.float32) ** block_levels(key_list[2], (NX, NY, CZ), ((0, 4), (1, 8)), -0.2, 0.2)), 0.5, 2.0),
    }


newton_shifts = (12.0, 3.0, 21.0, 7.0)
newton_scales = (8.0, 8.0, 8.0, 8.0)

def stencil_apply(field, coeff):
    field_z = jnp.pad(field, ((0, 0), (0, 0), (1, 1)))
    coeff_z = jnp.pad(coeff, ((0, 0), (0, 0), (1, 1)))
    center = field[1:-1, 1:-1]
    center_k = coeff[1:-1, 1:-1]
    beside_all = [(field[2:, 1:-1], coeff[2:, 1:-1]), (field[:-2, 1:-1], coeff[:-2, 1:-1]), (field[1:-1, 2:], coeff[1:-1, 2:]), (field[1:-1, :-2], coeff[1:-1, :-2]), (field_z[1:-1, 1:-1, 2:], coeff_z[1:-1, 1:-1, 2:]), (field_z[1:-1, 1:-1, :-2], coeff_z[1:-1, 1:-1, :-2])]
    total = jnp.zeros(center.shape, center.dtype)
    for other, other_k in beside_all:
        total = total + 0.5 * (center_k + other_k) * (center - other)
    return total

def padded(array):
    return jnp.pad(array, ((1, 1), (1, 1), (0, 0)))

def small_cholesky(matrix):
    order = matrix.shape[0]
    zero_val = matrix[0, 0] * 0.0
    lower = [[zero_val for col in range(order)] for row in range(order)]
    for col in range(order):
        diag_val = matrix[col, col]
        for inner in range(col):
            diag_val = diag_val - lower[col][inner] * lower[col][inner]
        lower[col][col] = jnp.sqrt(diag_val)
        for row in range(col + 1, order):
            entry = matrix[row, col]
            for inner in range(col):
                entry = entry - lower[row][inner] * lower[col][inner]
            lower[row][col] = entry / lower[col][col]
    return jnp.stack([jnp.stack(line) for line in lower])

def lower_inverse(lower):
    order = lower.shape[0]
    ident = jnp.eye(order, dtype=lower.dtype)
    result_rows = []
    for row in range(order):
        entry = ident[row]
        for inner in range(row):
            entry = entry - lower[row, inner] * result_rows[inner]
        result_rows.append(entry / lower[row, row])
    return jnp.stack(result_rows)

def upper_inverse(upper):
    order = upper.shape[0]
    ident = jnp.eye(order, dtype=upper.dtype)
    result_rows = [None] * order
    for row in range(order - 1, -1, -1):
        entry = ident[row]
        for inner in range(row + 1, order):
            entry = entry - upper[row, inner] * result_rows[inner]
        result_rows[row] = entry / upper[row, row]
    return jnp.stack(result_rows)

def gram_of(stacked):
    return lax.dot_general(stacked, stacked, (((1,), (1,)), ((), ())), precision=lax.Precision.HIGHEST)

def least_squares(rfactor):
    table = np.zeros((5, 4))
    for step in range(4):
        table[step, step] = newton_shifts[step]
        table[step + 1, step] = newton_scales[step]
    change = jnp.asarray(table, dtype=rfactor.dtype)
    upper_inv = upper_inverse(rfactor[:4, :4])
    hess = jnp.dot(jnp.dot(rfactor, change, precision=lax.Precision.HIGHEST), upper_inv, precision=lax.Precision.HIGHEST)
    normal_mat = jnp.dot(hess.T, hess, precision=lax.Precision.HIGHEST)
    target = rfactor[0, 0] * hess[0, :]
    factor_inv = lower_inverse(small_cholesky(normal_mat))
    middle = jnp.dot(factor_inv, target, precision=lax.Precision.HIGHEST)
    return jnp.dot(factor_inv.T, middle, precision=lax.Precision.HIGHEST)

def reference(right_side, initial, conduct):
    coeff_pad = padded(conduct)
    residual = right_side - stencil_apply(padded(initial), coeff_pad)
    vectors = [residual]
    for step in range(4):
        current = vectors[-1]
        vectors.append((stencil_apply(padded(current), coeff_pad) - newton_shifts[step] * current) / newton_scales[step])
    stacked = jnp.stack(vectors).reshape(5, -1)
    lower_one = small_cholesky(gram_of(stacked))
    first_q = jnp.dot(lower_inverse(lower_one), stacked, precision=lax.Precision.HIGHEST)
    lower_two = small_cholesky(gram_of(first_q))
    final_q = jnp.dot(lower_inverse(lower_two), first_q, precision=lax.Precision.HIGHEST)
    rfactor = jnp.dot(lower_two.T, lower_one.T, precision=lax.Precision.HIGHEST)
    weights = least_squares(rfactor)
    updated = initial + jnp.dot(weights, final_q[:4], precision=lax.Precision.HIGHEST).reshape(initial.shape)
    count = initial.shape[0] * initial.shape[1] * initial.shape[2]
    basis = (final_q * jnp.sqrt(jnp.float32(count)).astype(final_q.dtype)).reshape((5,) + initial.shape)
    return (basis, rfactor, updated)
```

```python
import functools
import math

import jax
import jax.numpy as jnp
from jax import lax
from jax.experimental import pallas as pl
from jax.experimental.pallas import tpu as pltpu
from jax.sharding import PartitionSpec as P

SHIFTS = (12.0, 3.0, 21.0, 7.0)
SCALE = 8.0
LANES = 128
MESH = pl.DeviceIdType.MESH
PAIRS = [(i, j) for j in range(5) for i in range(j + 1)]
F32 = jnp.float32


def inv_sqrt(value):
    guess = lax.rsqrt(value)
    return guess * (1.5 - 0.5 * (value * guess) * guess)


def cholesky(entry, order):
    lower, inv = {}, []
    for col in range(order):
        diag = entry(col, col)
        for inner in range(col):
            diag = diag - lower[col, inner] * lower[col, inner]
        root = inv_sqrt(diag)
        inv.append(root)
        lower[col, col] = diag * root
        for row in range(col + 1, order):
            val = entry(row, col)
            for inner in range(col):
                val = val - lower[row, inner] * lower[col, inner]
            lower[row, col] = val * root
    return lower, inv


def lower_inverse(lower, inv, order):
    result = {}
    for row in range(order):
        for col in range(row):
            total = lower[row, col] * result[col, col]
            for inner in range(col + 1, row):
                total = total + lower[row, inner] * result[inner, col]
            result[row, col] = -(total * inv[row])
        result[row, row] = inv[row]
    return result


def cycle_kernel(sizes, rs_hbm, init_hbm, cond_hbm, v_out, coef_out,
                 ku, rs, v0, v1, v2, v3, v4, cx, cy, cz, cfx, cfy, fy, hx, hy,
                 g1, g2, gm, load_sem, out_sem, hs_sem, hr_sem, s1, r1, s2, r2):
    nrows, ncols, nx, ny, nz = sizes
    nh = nz // LANES
    count = nx * ny
    step_rows = 2 * ny
    vecs = (v0, v1, v2, v3, v4)
    me_r, me_c = lax.axis_index("rows"), lax.axis_index("cols")

    loads = []
    for idx, (src, dst) in enumerate(((cond_hbm, ku.at[0]), (init_hbm, ku.at[1]), (rs_hbm, rs))):
        for h in range(nh):
            loads.append(pltpu.make_async_copy(
                src.at[:, pl.ds(h * LANES, LANES)], dst.at[h, pl.ds(0, count), :],
                load_sem.at[idx, h]))
            loads[-1].start()

    barrier = pltpu.get_barrier_semaphore()
    for d in range(1, ncols):
        pl.semaphore_signal(barrier, inc=1, device_id={"cols": lax.rem(me_c + d, ncols)},
                            device_id_type=MESH)
    for d in range(1, nrows):
        pl.semaphore_signal(barrier, inc=1, device_id={"rows": lax.rem(me_r + d, nrows)},
                            device_id_type=MESH)

    zero_plane = jnp.zeros((nh, ny, LANES), F32)
    for i in range(2):
        ku[i, :, pl.ds(count, ny), :] = zero_plane
    for vec in vecs[:4]:
        vec[:, pl.ds(count, ny), :] = zero_plane
    for edge, ref, side in ((me_c == 0, hy, 0), (me_c == ncols - 1, hy, 1),
                            (me_r == 0, hx, 0), (me_r == nrows - 1, hx, 1)):
        @pl.when(edge)
        def _(ref=ref, side=side):
            for k in range(6):
                ref[k, side] = jnp.zeros(ref.shape[2:], F32)

    def strided(side):
        return pl.ds(0 if side == 0 else ny - 1, nx, stride=ny)

    def face_copies(first, num, plane):
        made = []
        ks = first if num is None else pl.ds(first, num)
        for slot, axis, me, size in ((0, "cols", me_c, ncols), (1, "cols", me_c, ncols),
                                     (2, "rows", me_r, nrows), (3, "rows", me_r, nrows)):
            side = slot % 2
            target = me + 1 if side == 0 else me - 1
            has_target = me < size - 1 if side == 0 else me > 0
            has_source = me > 0 if side == 0 else me < size - 1
            if axis == "cols":
                src, dst = fy.at[ks, 1 - side], hy.at[ks, side]
            else:
                src, dst = plane(1 - side), hx.at[ks, side]
            made.append((has_target, has_source, pltpu.make_async_remote_copy(
                src_ref=src, dst_ref=dst, send_sem=hs_sem.at[first, slot],
                recv_sem=hr_sem.at[first, slot], device_id={axis: target}, device_id_type=MESH)))
        return made

    sent = []

    def send(copies):
        sent.extend(copies)
        for has_target, _, copy in copies:
            @pl.when(has_target)
            def _(copy=copy):
                copy.start()

    def arrive(copies):
        for _, has_source, copy in copies:
            @pl.when(has_source)
            def _(copy=copy):
                copy.wait_recv()

    def plane_start(side):
        return 0 if side == 0 else count - ny

    for cp in loads[:2 * nh]:
        cp.wait()
    for i in range(2):
        for side in range(2):
            for h in range(nh):
                fy[i, side, h] = ku[i, h, strided(side), :]
    pl.semaphore_wait(barrier, ncols + nrows - 2)
    first = face_copies(0, 2, lambda side: ku.at[:, :, pl.ds(plane_start(side), ny), :])
    send(first)

    def wide(ref, base, rows):
        return jnp.concatenate([ref[h, pl.ds(base, rows), :] for h in range(nh)], axis=1)

    def put(ref, base, rows, value):
        for h in range(nh):
            ref[h, pl.ds(base, rows), :] = value[:, h * LANES:(h + 1) * LANES]

    lane = lax.broadcasted_iota(jnp.int32, (step_rows, nz), 1)
    row = lax.broadcasted_iota(jnp.int32, (step_rows, nz), 0)
    sixteenth = 0.5 / SCALE
    y_mask = jnp.where(lax.rem(row, ny) == ny - 1, 0.0, sixteenth).astype(F32)
    z_mask = jnp.where(lane == nz - 1, 0.0, sixteenth).astype(F32)
    z_edge = jnp.where((lane == nz - 1) | (lane == 0), sixteenth, 0.0).astype(F32)
    kk, uu = ku.at[0], ku.at[1]

    @pl.loop(0, count // step_rows)
    def _(i):
        base = pl.multiple_of(i * step_rows, step_rows)
        here = wide(kk, base, step_rows)
        put(cx, base, step_rows, (here + wide(kk, base + ny, step_rows)) * sixteenth)
        put(cy, base, step_rows, (here + pltpu.roll(here, step_rows - 1, 0)) * y_mask)
        put(cz, base, step_rows, (here + pltpu.roll(here, nz - 1, 1)) * z_mask)
    cx[:, pl.ds(count - ny, ny), :] = zero_plane

    def interior(src, dst, shift, residual):
        def body(i, flux_before):
            base = pl.multiple_of(i * step_rows, step_rows)
            val = wide(src, base, step_rows)
            flux_x = wide(cx, base, step_rows) * (val - wide(src, base + ny, step_rows))
            total = flux_x - jnp.concatenate([flux_before, flux_x[:step_rows - ny]], axis=0)
            flux_y = wide(cy, base, step_rows) * (val - pltpu.roll(val, step_rows - 1, 0))
            total = total + (flux_y - pltpu.roll(flux_y, 1, 0))
            flux_z = wide(cz, base, step_rows) * (val - pltpu.roll(val, nz - 1, 1))
            total = total + (flux_z - pltpu.roll(flux_z, 1, 1))
            total = total + (wide(kk, base, step_rows) * z_edge - shift) * val
            if residual:
                total = wide(rs, base, step_rows) - SCALE * total
            put(dst, base, step_rows, total)
            return flux_x[step_rows - ny:]
        lax.fori_loop(0, count // step_rows, body, jnp.zeros((ny, nz), F32))

    def corrections(k, src, dst, sign, pack):
        for side in range(2):
            at = pl.ds(plane_start(side), ny)
            dst[:, at, :] = dst[:, at, :] + sign * (cfx[side] * (src[:, at, :] - hx[k, side]))
        for side in range(2):
            for h in range(nh):
                new = dst[h, strided(side), :] + sign * (
                    cfy[side, h] * (fy[k, side, h] - hy[k, side, h]))
                dst[h, strided(side), :] = new
                if pack:
                    fy[k + 1, side, h] = new

    for cp in loads[2 * nh:]:
        cp.wait()
    interior(uu, v0, 0.0, True)
    arrive(first)
    for side in range(2):
        at = pl.ds(plane_start(side), ny)
        cfx[side] = (kk[:, at, :] + hx[0, side]) * sixteenth
        cfy[side] = (fy[0, side] + hy[0, side]) * sixteenth
    corrections(1, uu, v0, -SCALE, True)

    sums = {}

    def gram_with(k):
        def body(i, accs):
            base = pl.multiple_of(i * 16, 16)
            accs = list(accs)
            for h in range(nh):
                for sub in range(2):
                    at = pl.ds(base + 8 * sub, 8)
                    mine = vecs[k][h, at, :]
                    for j in range(k + 1):
                        other = mine if j == k else vecs[j][h, at, :]
                        accs[j] = accs[j] + mine * other
            return tuple(accs)
        accs = lax.fori_loop(0, count // 16, body,
                             tuple(jnp.zeros((8, LANES), F32) for _ in range(k + 1)), unroll=2)
        for j in range(k + 1):
            sums[j, k] = accs[j]

    outs = []

    def write_out(k):
        for h in range(nh):
            outs.append(pltpu.make_async_copy(
                vecs[k].at[h, pl.ds(0, count), :], v_out.at[k, :, pl.ds(h * LANES, LANES)],
                out_sem.at[k, h]))
            outs[-1].start()

    for k in range(4):
        vec = vecs[k]
        copies = face_copies(2 + k, None,
                             lambda side, vec=vec: vec.at[:, pl.ds(plane_start(side), ny), :])
        send(copies)
        write_out(k)
        interior(vec, vecs[k + 1], SHIFTS[k] / SCALE, False)
        gram_with(k)
        arrive(copies)
        corrections(2 + k, vec, vecs[k + 1], 1.0, k < 3)
    write_out(4)
    gram_with(4)

    def exchange(p, buf, me, size, axis, ssem, rsem, value):
        buf[p, me] = value
        for d in range(1, size):
            copy = pltpu.make_async_remote_copy(
                src_ref=buf.at[p, me], dst_ref=buf.at[p, me], send_sem=ssem.at[p, d],
                recv_sem=rsem.at[p, d], device_id={axis: lax.rem(me + d, size)},
                device_id_type=MESH)
            copy.start()
            sent.append((None, None, copy))
        for d in range(1, size):
            slot = lax.rem(me + size - d, size)
            pltpu.make_async_remote_copy(
                src_ref=buf.at[p, me], dst_ref=buf.at[p, slot], send_sem=ssem.at[p, d],
                recv_sem=rsem.at[p, d], device_id={axis: slot}, device_id_type=MESH).wait_recv()
        total = buf[p, 0]
        for i in range(1, size):
            total = total + buf[p, i]
        return total

    def all_reduce(p, values):
        for e, pair in enumerate(PAIRS):
            gm[e:e + 1, :] = jnp.sum(values[pair], axis=0, keepdims=True)
        part = exchange(p, g1, me_c, ncols, "cols", s1, r1, gm[...])
        part = exchange(p, g2, me_r, nrows, "rows", s2, r2, part)
        gm[...] = jnp.broadcast_to(jnp.sum(part, axis=1, keepdims=True), gm.shape)
        full = {pair: gm[e:e + 1, :] for e, pair in enumerate(PAIRS)}
        return lambda i, j: full[j, i]

    gm[...] = jnp.zeros(gm.shape, F32)
    low_one, inv_one = cholesky(all_reduce(0, sums), 5)
    linv_one = lower_inverse(low_one, inv_one, 5)
    splat = {key: jnp.broadcast_to(val, (8, LANES)) for key, val in linv_one.items()}

    def body(i, accs):
        base = pl.multiple_of(i * 16, 16)
        accs = list(accs)
        for h in range(nh):
            for sub in range(2):
                at = pl.ds(base + 8 * sub, 8)
                raw = [vec[h, at, :] for vec in vecs]
                ortho = []
                for r in range(5):
                    val = splat[r, 0] * raw[0]
                    for c in range(1, r + 1):
                        val = val + splat[r, c] * raw[c]
                    ortho.append(val)
                for e, (a, b) in enumerate(PAIRS):
                    accs[e] = accs[e] + ortho[a] * ortho[b]
        return tuple(accs)
    accs = lax.fori_loop(0, count // 16, body, tuple(jnp.zeros((8, LANES), F32) for _ in PAIRS))

    low_two, inv_two = cholesky(all_reduce(1, dict(zip(PAIRS, accs))), 5)
    linv_two = lower_inverse(low_two, inv_two, 5)

    def add_up(terms):
        return functools.reduce(lambda a, b: a + b, terms)

    trans = {(i, j): add_up([linv_two[i, m] * linv_one[m, j] for m in range(j, i + 1)])
             for i in range(5) for j in range(i + 1)}
    rfac = {(i, j): add_up([low_two[m, i] * low_one[j, m] for m in range(i, j + 1)])
            for i in range(5) for j in range(i, 5)}
    shifted = {}
    for k in range(4):
        for i in range(k + 2):
            val = rfac[i, k + 1] * SCALE
            shifted[i, k] = val + rfac[i, k] * SHIFTS[k] if i <= k else val
    hess = {(i, k): add_up([shifted[i, m] * trans[k, m] for m in range(max(i - 1, 0), k + 1)])
            for k in range(4) for i in range(k + 2)}
    normal = {(i, j): add_up([hess[m, i] * hess[m, j] for m in range(min(i, j) + 2)])
              for i in range(4) for j in range(i + 1)}
    low_n, inv_n = cholesky(lambda i, j: normal[i, j], 4)
    middle = []
    for i in range(4):
        val = rfac[0, 0] * hess[0, i]
        for m in range(i):
            val = val - low_n[i, m] * middle[m]
        middle.append(val * inv_n[i])
    weights = [None] * 4
    for i in range(3, -1, -1):
        val = middle[i]
        for m in range(i + 1, 4):
            val = val - low_n[m, i] * weights[m]
        weights[i] = val * inv_n[i]

    root = math.sqrt(nrows * ncols * nx * ny * nz)
    for e, (j, i) in enumerate(PAIRS):
        coef_out[e:e + 1, :] = trans[i, j] * root
    for k in range(4):
        coef_out[16 + k:17 + k, :] = weights[k] * (1.0 / root)
    one_row = lax.broadcasted_iota(jnp.int32, (1, LANES), 1)
    for i in range(5):
        line = jnp.zeros((1, LANES), F32)
        for j in range(i, 5):
            line = jnp.where(one_row == j, rfac[i, j], line)
        coef_out[24 + i:25 + i, :] = line

    for cp in outs:
        cp.wait()
    for has_target, _, copy in sent:
        if has_target is None:
            copy.wait_send()
        else:
            @pl.when(has_target)
            def _(copy=copy):
                copy.wait_send()


def finish_kernel(v_ref, init_ref, coef_ref, basis_ref, rfac_ref, updated_ref):
    rows, nz = init_ref.shape
    trans = {(i, j): jnp.broadcast_to(coef_ref[e:e + 1, :], (8, LANES))
             for e, (j, i) in enumerate(PAIRS)}
    weights = [jnp.broadcast_to(coef_ref[16 + k:17 + k, :], (8, LANES)) for k in range(4)]

    def body(n, carry):
        at = pl.ds(pl.multiple_of(n * 8, 8), 8)
        for h in range(nz // LANES):
            lanes = pl.ds(h * LANES, LANES)
            raw = [v_ref[k, at, lanes] for k in range(5)]
            new = init_ref[at, lanes]
            for i in range(5):
                val = trans[i, 0] * raw[0]
                for j in range(1, i + 1):
                    val = val + trans[i, j] * raw[j]
                basis_ref[i, at, lanes] = val
                if i < 4:
                    new = new + weights[i] * val
            updated_ref[at, lanes] = new
        return carry
    lax.fori_loop(0, rows // 8, body, 0, unroll=2)
    rfac_ref[...] = coef_ref[24:29, 0:5]


def on_device(nrows, ncols, right_side, initial, conduct):
    nx, ny, nz = initial.shape
    nh, count = nz // LANES, nx * ny
    flat = [a.reshape(count, nz) for a in (right_side, initial, conduct)]
    dma = pltpu.SemaphoreType.DMA
    vec = pltpu.VMEM((nh, count + ny, LANES), F32)
    plain = pltpu.VMEM((nh, count, LANES), F32)
    vectors, coefs = pl.pallas_call(
        functools.partial(cycle_kernel, (nrows, ncols, nx, ny, nz)),
        out_shape=(jax.ShapeDtypeStruct((5, count, nz), F32),
                   jax.ShapeDtypeStruct((32, LANES), F32)),
        in_specs=[pl.BlockSpec(memory_space=pl.ANY)] * 3,
        out_specs=(pl.BlockSpec(memory_space=pl.ANY), pl.BlockSpec(memory_space=pltpu.VMEM)),
        scratch_shapes=[
            pltpu.VMEM((2, nh, count + ny, LANES), F32), plain, vec, vec, vec, vec, plain,
            plain, plain, plain,
            pltpu.VMEM((2, nh, ny, LANES), F32), pltpu.VMEM((2, nh, nx, LANES), F32),
            pltpu.VMEM((6, 2, nh, nx, LANES), F32),
            pltpu.VMEM((6, 2, nh, ny, LANES), F32), pltpu.VMEM((6, 2, nh, nx, LANES), F32),
            pltpu.VMEM((2, ncols, 16, LANES), F32), pltpu.VMEM((2, nrows, 16, LANES), F32),
            pltpu.VMEM((16, LANES), F32),
            dma((3, nh)), dma((5, nh)), dma((6, 4)), dma((6, 4)),
            dma((2, ncols)), dma((2, ncols)), dma((2, nrows)), dma((2, nrows)),
        ],
        compiler_params=pltpu.CompilerParams(
            collective_id=0, has_side_effects=True, vmem_limit_bytes=40 << 20),
        name="cycle",
    )(*flat)
    block = 128
    basis, rfactor, updated = pl.pallas_call(
        finish_kernel,
        grid=(count // block,),
        out_shape=(jax.ShapeDtypeStruct((5, count, nz), F32),
                   jax.ShapeDtypeStruct((5, 5), F32),
                   jax.ShapeDtypeStruct((count, nz), F32)),
        in_specs=[pl.BlockSpec((5, block, nz), lambda i: (0, i, 0)),
                  pl.BlockSpec((block, nz), lambda i: (i, 0)),
                  pl.BlockSpec((32, LANES), lambda i: (0, 0))],
        out_specs=(pl.BlockSpec((5, block, nz), lambda i: (0, i, 0)),
                   pl.BlockSpec((5, 5), lambda i: (0, 0)),
                   pl.BlockSpec((block, nz), lambda i: (i, 0))),
        compiler_params=pltpu.CompilerParams(vmem_limit_bytes=40 << 20),
        name="finish",
    )(vectors, flat[1], coefs)
    return (basis.reshape(5, nx, ny, nz), rfactor, updated.reshape(nx, ny, nz))


def solution(mesh):
    nrows, ncols = mesh.shape["rows"], mesh.shape["cols"]
    return jax.shard_map(
        functools.partial(on_device, nrows, ncols),
        mesh=mesh,
        in_specs=(P("rows", "cols", None),) * 3,
        out_specs=(P(None, "rows", "cols", None), P(), P("rows", "cols", None)),
        check_vma=False,
    )
```

```python
import functools
import math

import jax
import jax.numpy as jnp
from jax import lax
from jax.experimental import pallas as pl
from jax.experimental.pallas import tpu as pltpu
from jax.sharding import PartitionSpec as P

SHIFTS = (12.0, 3.0, 21.0, 7.0)
SCALE = 8.0
LANES = 128
MESH = pl.DeviceIdType.MESH
PAIRS = [(i, j) for j in range(5) for i in range(j + 1)]
F32 = jnp.float32


def inv_sqrt(value):
    guess = lax.rsqrt(value)
    return guess * (1.5 - 0.5 * (value * guess) * guess)


def cholesky(entry, order):
    lower, inv = {}, []
    for col in range(order):
        diag = entry(col, col)
        for inner in range(col):
            diag = diag - lower[col, inner] * lower[col, inner]
        root = inv_sqrt(diag)
        inv.append(root)
        lower[col, col] = diag * root
        for row in range(col + 1, order):
            val = entry(row, col)
            for inner in range(col):
                val = val - lower[row, inner] * lower[col, inner]
            lower[row, col] = val * root
    return lower, inv


def lower_inverse(lower, inv, order):
    result = {}
    for row in range(order):
        for col in range(row):
            total = lower[row, col] * result[col, col]
            for inner in range(col + 1, row):
                total = total + lower[row, inner] * result[inner, col]
            result[row, col] = -(total * inv[row])
        result[row, row] = inv[row]
    return result


def cycle_kernel(sizes, rs_hbm, init_hbm, cond_hbm, v_out, coef_out,
                 ku, rs, v0, v1, v2, v3, v4, cx, cy, cyb, cz, czb, cfx, cfy, fy, hx, hy,
                 g1, g2, gm, load_sem, out_sem, hs_sem, hr_sem, s1, r1, s2, r2):
    nrows, ncols, nx, ny, nz = sizes
    nh = nz // LANES
    count = nx * ny
    step_rows = 4 * ny
    one_stage = nrows * ncols <= 64
    vecs = (v0, v1, v2, v3, v4)
    me_r, me_c = lax.axis_index("rows"), lax.axis_index("cols")

    loads = []
    for idx, (src, dst) in enumerate(((cond_hbm, ku.at[0]), (init_hbm, ku.at[1]), (rs_hbm, rs))):
        for h in range(nh):
            loads.append(pltpu.make_async_copy(
                src.at[:, pl.ds(h * LANES, LANES)], dst.at[h, pl.ds(0, count), :],
                load_sem.at[idx, h]))
            loads[-1].start()

    barrier = pltpu.get_barrier_semaphore()
    everyone = [(dr, dc) for dr in range(nrows) for dc in range(ncols)][1:]
    greeted = everyone if one_stage else (
        [(0, d) for d in range(1, ncols)] + [(d, 0) for d in range(1, nrows)])
    for dr, dc in greeted:
        pl.semaphore_signal(barrier, inc=1, device_id_type=MESH,
                            device_id=(lax.rem(me_r + dr, nrows), lax.rem(me_c + dc, ncols)))

    zero_plane = jnp.zeros((nh, ny, LANES), F32)
    for i in range(2):
        ku[i, :, pl.ds(count, ny), :] = zero_plane
    for vec in vecs[:4]:
        vec[:, pl.ds(count, ny), :] = zero_plane
    for edge, ref, side in ((me_c == 0, hy, 0), (me_c == ncols - 1, hy, 1),
                            (me_r == 0, hx, 0), (me_r == nrows - 1, hx, 1)):
        @pl.when(edge)
        def _(ref=ref, side=side):
            for k in range(6):
                ref[k, side] = jnp.zeros(ref.shape[2:], F32)

    def strided(side):
        return pl.ds(0 if side == 0 else ny - 1, nx, stride=ny)

    def face_copies(first, num, plane):
        made = []
        ks = first if num is None else pl.ds(first, num)
        for slot, axis, me, size in ((0, "cols", me_c, ncols), (1, "cols", me_c, ncols),
                                     (2, "rows", me_r, nrows), (3, "rows", me_r, nrows)):
            side = slot % 2
            target = me + 1 if side == 0 else me - 1
            has_target = me < size - 1 if side == 0 else me > 0
            has_source = me > 0 if side == 0 else me < size - 1
            if axis == "cols":
                src, dst = fy.at[ks, 1 - side], hy.at[ks, side]
            else:
                src, dst = plane(1 - side), hx.at[ks, side]
            made.append((has_target, has_source, pltpu.make_async_remote_copy(
                src_ref=src, dst_ref=dst, send_sem=hs_sem.at[first, slot],
                recv_sem=hr_sem.at[first, slot], device_id={axis: target}, device_id_type=MESH)))
        return made

    sent = []

    def send(copies):
        sent.extend(copies)
        for has_target, _, copy in copies:
            @pl.when(has_target)
            def _(copy=copy):
                copy.start()

    def arrive(copies):
        for _, has_source, copy in copies:
            @pl.when(has_source)
            def _(copy=copy):
                copy.wait_recv()

    def plane_start(side):
        return 0 if side == 0 else count - ny

    for cp in loads[:2 * nh]:
        cp.wait()
    for i in range(2):
        for side in range(2):
            for h in range(nh):
                fy[i, side, h] = ku[i, h, strided(side), :]
    pl.semaphore_wait(barrier, len(greeted))
    first = face_copies(0, 2, lambda side: ku.at[:, :, pl.ds(plane_start(side), ny), :])
    send(first)

    def wide(ref, base, rows):
        return jnp.concatenate([ref[h, pl.ds(base, rows), :] for h in range(nh)], axis=1)

    def put(ref, base, rows, value):
        for h in range(nh):
            ref[h, pl.ds(base, rows), :] = value[:, h * LANES:(h + 1) * LANES]

    lane = lax.broadcasted_iota(jnp.int32, (step_rows, nz), 1)
    row = lax.broadcasted_iota(jnp.int32, (step_rows, nz), 0)
    sixteenth = 0.5 / SCALE
    y_mask = jnp.where(lax.rem(row, ny) == ny - 1, 0.0, sixteenth).astype(F32)
    z_mask = jnp.where(lane == nz - 1, 0.0, sixteenth).astype(F32)
    z_edge = jnp.where((lane == nz - 1) | (lane == 0), sixteenth, 0.0).astype(F32)
    kk, uu = ku.at[0], ku.at[1]

    @pl.loop(0, count // step_rows)
    def _(i):
        base = pl.multiple_of(i * step_rows, step_rows)
        here = wide(kk, base, step_rows)
        put(cx, base, step_rows, (here + wide(kk, base + ny, step_rows)) * sixteenth)
        above = (here + pltpu.roll(here, step_rows - 1, 0)) * y_mask
        put(cy, base, step_rows, above)
        put(cyb, base, step_rows, pltpu.roll(above, 1, 0))
        after = (here + pltpu.roll(here, nz - 1, 1)) * z_mask
        put(cz, base, step_rows, after)
        put(czb, base, step_rows, pltpu.roll(after, 1, 1))
    cx[:, pl.ds(count - ny, ny), :] = zero_plane

    def interior(src, dst, shift, residual):
        def body(i, flux_before):
            base = pl.multiple_of(i * step_rows, step_rows)
            val = wide(src, base, step_rows)
            flux_x = wide(cx, base, step_rows) * (val - wide(src, base + ny, step_rows))
            total = flux_x - jnp.concatenate([flux_before, flux_x[:step_rows - ny]], axis=0)
            total = total + wide(cy, base, step_rows) * (val - pltpu.roll(val, step_rows - 1, 0))
            total = total + wide(cyb, base, step_rows) * (val - pltpu.roll(val, 1, 0))
            total = total + wide(cz, base, step_rows) * (val - pltpu.roll(val, nz - 1, 1))
            total = total + wide(czb, base, step_rows) * (val - pltpu.roll(val, 1, 1))
            total = total + (wide(kk, base, step_rows) * z_edge - shift) * val
            if residual:
                total = wide(rs, base, step_rows) - SCALE * total
            put(dst, base, step_rows, total)
            return flux_x[step_rows - ny:]
        lax.fori_loop(0, count // step_rows, body, jnp.zeros((ny, nz), F32))

    def corrections(k, src, dst, sign, pack):
        for side in range(2):
            at = pl.ds(plane_start(side), ny)
            dst[:, at, :] = dst[:, at, :] + sign * (cfx[side] * (src[:, at, :] - hx[k, side]))
        for side in range(2):
            for h in range(nh):
                new = dst[h, strided(side), :] + sign * (
                    cfy[side, h] * (fy[k, side, h] - hy[k, side, h]))
                dst[h, strided(side), :] = new
                if pack:
                    fy[k + 1, side, h] = new

    for cp in loads[2 * nh:]:
        cp.wait()
    interior(uu, v0, 0.0, True)
    arrive(first)
    for side in range(2):
        at = pl.ds(plane_start(side), ny)
        cfx[side] = (kk[:, at, :] + hx[0, side]) * sixteenth
        cfy[side] = (fy[0, side] + hy[0, side]) * sixteenth
    corrections(1, uu, v0, -SCALE, True)

    sums = {}

    def gram_with(k):
        def body(i, accs):
            base = pl.multiple_of(i * 16, 16)
            accs = list(accs)
            for h in range(nh):
                for sub in range(2):
                    at = pl.ds(base + 8 * sub, 8)
                    mine = vecs[k][h, at, :]
                    for j in range(k + 1):
                        other = mine if j == k else vecs[j][h, at, :]
                        accs[j] = accs[j] + mine * other
            return tuple(accs)
        accs = lax.fori_loop(0, count // 16, body,
                             tuple(jnp.zeros((8, LANES), F32) for _ in range(k + 1)), unroll=2)
        for j in range(k + 1):
            sums[j, k] = accs[j]

    outs = []

    def write_out(k):
        for h in range(nh):
            outs.append(pltpu.make_async_copy(
                vecs[k].at[h, pl.ds(0, count), :], v_out.at[k, :, pl.ds(h * LANES, LANES)],
                out_sem.at[k, h]))
            outs[-1].start()

    for k in range(4):
        vec = vecs[k]
        copies = face_copies(2 + k, None,
                             lambda side, vec=vec: vec.at[:, pl.ds(plane_start(side), ny), :])
        send(copies)
        write_out(k)
        interior(vec, vecs[k + 1], SHIFTS[k] / SCALE, False)
        gram_with(k)
        arrive(copies)
        corrections(2 + k, vec, vecs[k + 1], 1.0, k < 3)
    write_out(4)
    gram_with(4)

    def exchange(p, buf, ssem, rsem, peers, slot, value):
        buf[p, slot(0, 0)] = value
        for e, (dr, dc) in enumerate(peers):
            copy = pltpu.make_async_remote_copy(
                src_ref=buf.at[p, slot(0, 0)], dst_ref=buf.at[p, slot(0, 0)],
                send_sem=ssem.at[p, e], recv_sem=rsem.at[p, e],
                device_id=(lax.rem(me_r + dr, nrows), lax.rem(me_c + dc, ncols)),
                device_id_type=MESH)
            copy.start()
            sent.append((None, None, copy))
        for e, (dr, dc) in enumerate(peers):
            pltpu.make_async_remote_copy(
                src_ref=buf.at[p, slot(0, 0)], dst_ref=buf.at[p, slot(nrows - dr, ncols - dc)],
                send_sem=ssem.at[p, e], recv_sem=rsem.at[p, e],
                device_id=(lax.rem(me_r + nrows - dr, nrows), lax.rem(me_c + ncols - dc, ncols)),
                device_id_type=MESH).wait_recv()
        parts = [buf[p, i] for i in range(len(peers) + 1)]
        while len(parts) > 1:
            parts = [a + b for a, b in zip(parts[::2], parts[1::2])] + (
                parts[-1:] if len(parts) % 2 else [])
        return parts[0]

    def col_of(dc):
        return lax.rem(me_c + dc, ncols)

    def row_of(dr):
        return lax.rem(me_r + dr, nrows)

    pair_row = lax.broadcasted_iota(jnp.int32, (16, LANES), 0)
    on_diag = pair_row == lax.broadcasted_iota(jnp.int32, (16, LANES), 1)

    def all_reduce(p, values):
        for e, pair in enumerate(PAIRS):
            gm[e:e + 1, :] = jnp.sum(values[pair], axis=0, keepdims=True)
        line = jnp.sum(jnp.where(on_diag, jnp.sum(gm[...], axis=1, keepdims=True), 0.0),
                       axis=0, keepdims=True)
        if one_stage:
            line = exchange(p, g1, s1, r1, everyone,
                            lambda dr, dc: row_of(dr) * ncols + col_of(dc), line)
        else:
            line = exchange(p, g1, s1, r1, [(0, d) for d in range(1, ncols)],
                            lambda dr, dc: col_of(dc), line)
            line = exchange(p, g2, s2, r2, [(d, 0) for d in range(1, nrows)],
                            lambda dr, dc: row_of(dr), line)
        gm[...] = jnp.broadcast_to(
            jnp.sum(jnp.where(on_diag, line, 0.0), axis=1, keepdims=True), gm.shape)
        full = {pair: gm[e:e + 1, :] for e, pair in enumerate(PAIRS)}
        return lambda i, j: full[j, i]

    gm[...] = jnp.zeros(gm.shape, F32)
    low_one, inv_one = cholesky(all_reduce(0, sums), 5)
    linv_one = lower_inverse(low_one, inv_one, 5)
    splat = {key: jnp.broadcast_to(val, (8, LANES)) for key, val in linv_one.items()}

    def body(i, accs):
        base = pl.multiple_of(i * 16, 16)
        accs = list(accs)
        for h in range(nh):
            for sub in range(2):
                at = pl.ds(base + 8 * sub, 8)
                raw = [vec[h, at, :] for vec in vecs]
                ortho = []
                for r in range(5):
                    val = splat[r, 0] * raw[0]
                    for c in range(1, r + 1):
                        val = val + splat[r, c] * raw[c]
                    ortho.append(val)
                for e, (a, b) in enumerate(PAIRS):
                    accs[e] = accs[e] + ortho[a] * ortho[b]
        return tuple(accs)
    accs = lax.fori_loop(0, count // 16, body, tuple(jnp.zeros((8, LANES), F32) for _ in PAIRS), unroll=2)

    low_two, inv_two = cholesky(all_reduce(1, dict(zip(PAIRS, accs))), 5)
    linv_two = lower_inverse(low_two, inv_two, 5)

    def add_up(terms):
        return functools.reduce(lambda a, b: a + b, terms)

    trans = {(i, j): add_up([linv_two[i, m] * linv_one[m, j] for m in range(j, i + 1)])
             for i in range(5) for j in range(i + 1)}
    rfac = {(i, j): add_up([low_two[m, i] * low_one[j, m] for m in range(i, j + 1)])
            for i in range(5) for j in range(i, 5)}
    shifted = {}
    for k in range(4):
        for i in range(k + 2):
            val = rfac[i, k + 1] * SCALE
            shifted[i, k] = val + rfac[i, k] * SHIFTS[k] if i <= k else val
    hess = {(i, k): add_up([shifted[i, m] * trans[k, m] for m in range(max(i - 1, 0), k + 1)])
            for k in range(4) for i in range(k + 2)}
    target, inv_n = [rfac[0, 0]], []
    for k in range(4):
        top, bottom = hess[k, k], hess[k + 1, k]
        square = top * top + bottom * bottom
        inv_n.append(inv_sqrt(square))
        cosine, sine = top * inv_n[k], bottom * inv_n[k]
        for j in range(k + 1, 4):
            upper, under = hess[k, j], hess[k + 1, j]
            hess[k, j] = cosine * upper + sine * under
            hess[k + 1, j] = cosine * under - sine * upper
        target.append(-(sine * target[k]))
        target[k] = cosine * target[k]
    weights = [None] * 4
    for i in range(3, -1, -1):
        val = target[i]
        for m in range(i + 1, 4):
            val = val - hess[i, m] * weights[m]
        weights[i] = val * inv_n[i]

    root = math.sqrt(nrows * ncols * nx * ny * nz)
    for e, (j, i) in enumerate(PAIRS):
        coef_out[e:e + 1, :] = trans[i, j] * root
    for k in range(4):
        coef_out[16 + k:17 + k, :] = weights[k] * (1.0 / root)
    one_row = lax.broadcasted_iota(jnp.int32, (1, LANES), 1)
    for i in range(5):
        line = jnp.zeros((1, LANES), F32)
        for j in range(i, 5):
            line = jnp.where(one_row == j, rfac[i, j], line)
        coef_out[24 + i:25 + i, :] = line

    for cp in outs:
        cp.wait()
    for has_target, _, copy in sent:
        if has_target is None:
            copy.wait_send()
        else:
            @pl.when(has_target)
            def _(copy=copy):
                copy.wait_send()


def finish_kernel(v_ref, init_ref, coef_ref, basis_ref, rfac_ref, updated_ref):
    rows, nz = init_ref.shape
    trans = {(i, j): jnp.broadcast_to(coef_ref[e:e + 1, :], (8, LANES))
             for e, (j, i) in enumerate(PAIRS)}
    weights = [jnp.broadcast_to(coef_ref[16 + k:17 + k, :], (8, LANES)) for k in range(4)]

    def body(n, carry):
        at = pl.ds(pl.multiple_of(n * 8, 8), 8)
        for h in range(nz // LANES):
            lanes = pl.ds(h * LANES, LANES)
            raw = [v_ref[k, at, lanes] for k in range(5)]
            new = init_ref[at, lanes]
            for i in range(5):
                val = trans[i, 0] * raw[0]
                for j in range(1, i + 1):
                    val = val + trans[i, j] * raw[j]
                basis_ref[i, at, lanes] = val
                if i < 4:
                    new = new + weights[i] * val
            updated_ref[at, lanes] = new
        return carry
    lax.fori_loop(0, rows // 8, body, 0, unroll=4)
    rfac_ref[...] = coef_ref[24:29, 0:5]


def on_device(nrows, ncols, right_side, initial, conduct):
    nx, ny, nz = initial.shape
    nh, count = nz // LANES, nx * ny
    flat = [a.reshape(count, nz) for a in (right_side, initial, conduct)]
    dma = pltpu.SemaphoreType.DMA
    slots = nrows * ncols
    vec = pltpu.VMEM((nh, count + ny, LANES), F32)
    plain = pltpu.VMEM((nh, count, LANES), F32)
    vectors, coefs = pl.pallas_call(
        functools.partial(cycle_kernel, (nrows, ncols, nx, ny, nz)),
        out_shape=(jax.ShapeDtypeStruct((5, count, nz), F32),
                   jax.ShapeDtypeStruct((32, LANES), F32)),
        in_specs=[pl.BlockSpec(memory_space=pltpu.HBM)] * 3,
        out_specs=(pl.BlockSpec(memory_space=pl.ANY), pl.BlockSpec(memory_space=pltpu.VMEM)),
        scratch_shapes=[
            pltpu.VMEM((2, nh, count + ny, LANES), F32), plain, vec, vec, vec, vec, plain,
            plain, plain, plain, plain, plain,
            pltpu.VMEM((2, nh, ny, LANES), F32), pltpu.VMEM((2, nh, nx, LANES), F32),
            pltpu.VMEM((6, 2, nh, nx, LANES), F32),
            pltpu.VMEM((6, 2, nh, ny, LANES), F32), pltpu.VMEM((6, 2, nh, nx, LANES), F32),
            pltpu.VMEM((2, slots, 1, LANES), F32), pltpu.VMEM((2, nrows, 1, LANES), F32),
            pltpu.VMEM((16, LANES), F32),
            dma((3, nh)), dma((5, nh)), dma((6, 4)), dma((6, 4)),
            dma((2, slots)), dma((2, slots)), dma((2, nrows)), dma((2, nrows)),
        ],
        compiler_params=pltpu.CompilerParams(
            collective_id=0, has_side_effects=True, vmem_limit_bytes=60 << 20),
        name="cycle",
    )(*flat)
    block = 256
    basis, rfactor, updated = pl.pallas_call(
        finish_kernel,
        grid=(count // block,),
        out_shape=(jax.ShapeDtypeStruct((5, count, nz), F32),
                   jax.ShapeDtypeStruct((5, 5), F32),
                   jax.ShapeDtypeStruct((count, nz), F32)),
        in_specs=[pl.BlockSpec((5, block, nz), lambda i: (0, i, 0)),
                  pl.BlockSpec((block, nz), lambda i: (i, 0)),
                  pl.BlockSpec((32, LANES), lambda i: (0, 0))],
        out_specs=(pl.BlockSpec((5, block, nz), lambda i: (0, i, 0)),
                   pl.BlockSpec((5, 5), lambda i: (0, 0)),
                   pl.BlockSpec((block, nz), lambda i: (i, 0))),
        compiler_params=pltpu.CompilerParams(vmem_limit_bytes=60 << 20),
        name="finish",
    )(vectors, flat[1], coefs)
    return (basis.reshape(5, nx, ny, nz), rfactor, updated.reshape(nx, ny, nz))


def solution(mesh):
    nrows, ncols = mesh.shape["rows"], mesh.shape["cols"]
    return jax.shard_map(
        functools.partial(on_device, nrows, ncols),
        mesh=mesh,
        in_specs=(P("rows", "cols", None),) * 3,
        out_specs=(P(None, "rows", "cols", None), P(), P("rows", "cols", None)),
        check_vma=False,
    )
```

```python
import functools
import math

import jax
import jax.numpy as jnp
from jax import lax
from jax.experimental import pallas as pl
from jax.experimental.pallas import tpu as pltpu
from jax.sharding import PartitionSpec as P

SHIFTS = (12.0, 3.0, 21.0, 7.0)
SCALE = 8.0
LANES = 128
MESH = pl.DeviceIdType.MESH
PAIRS = [(i, j) for j in range(5) for i in range(j + 1)]
F32 = jnp.float32


def inv_sqrt(value):
    guess = lax.rsqrt(value)
    return guess * (1.5 - 0.5 * (value * guess) * guess)


def cholesky(entry, order):
    lower, inv = {}, []
    for col in range(order):
        diag = entry(col, col)
        for inner in range(col):
            diag = diag - lower[col, inner] * lower[col, inner]
        root = inv_sqrt(diag)
        inv.append(root)
        lower[col, col] = diag * root
        for row in range(col + 1, order):
            val = entry(row, col)
            for inner in range(col):
                val = val - lower[row, inner] * lower[col, inner]
            lower[row, col] = val * root
    return lower, inv


def lower_inverse(lower, inv, order):
    result = {}
    for row in range(order):
        for col in range(row):
            total = lower[row, col] * result[col, col]
            for inner in range(col + 1, row):
                total = total + lower[row, inner] * result[inner, col]
            result[row, col] = -(total * inv[row])
        result[row, row] = inv[row]
    return result


def cycle_kernel(sizes, rs_hbm, init_hbm, cond_hbm, v_out, coef_out,
                 ku, rs, v0, v1, v2, v3, v4, cx, cy, cyb, cz, czb, cfx, cfy, fy, hx, hy,
                 g1, g2, gm, load_sem, out_sem, hs_sem, hr_sem, s1, r1, s2, r2):
    nrows, ncols, nx, ny, nz = sizes
    nh = nz // LANES
    count = nx * ny
    step_rows = 4 * ny
    one_stage = nrows * ncols <= 64
    vecs = (v0, v1, v2, v3, v4)
    me_r, me_c = lax.axis_index("rows"), lax.axis_index("cols")

    loads = []
    for idx, (src, dst) in enumerate(((cond_hbm, ku.at[0]), (init_hbm, ku.at[1]), (rs_hbm, rs))):
        for h in range(nh):
            loads.append(pltpu.make_async_copy(
                src.at[:, pl.ds(h * LANES, LANES)], dst.at[h, pl.ds(0, count), :],
                load_sem.at[idx, h]))
            loads[-1].start()

    barrier = pltpu.get_barrier_semaphore()
    everyone = [(dr, dc) for dr in range(nrows) for dc in range(ncols)][1:]
    greeted = everyone if one_stage else (
        [(0, d) for d in range(1, ncols)] + [(d, 0) for d in range(1, nrows)])
    for dr, dc in greeted:
        pl.semaphore_signal(barrier, inc=1, device_id_type=MESH,
                            device_id=(lax.rem(me_r + dr, nrows), lax.rem(me_c + dc, ncols)))

    zero_plane = jnp.zeros((nh, ny, LANES), F32)
    for i in range(2):
        ku[i, :, pl.ds(count, ny), :] = zero_plane
    for vec in vecs[:4]:
        vec[:, pl.ds(count, ny), :] = zero_plane
    for edge, ref, side in ((me_c == 0, hy, 0), (me_c == ncols - 1, hy, 1),
                            (me_r == 0, hx, 0), (me_r == nrows - 1, hx, 1)):
        @pl.when(edge)
        def _(ref=ref, side=side):
            for k in range(6):
                ref[k, side] = jnp.zeros(ref.shape[2:], F32)

    def strided(side):
        return pl.ds(0 if side == 0 else ny - 1, nx, stride=ny)

    def face_copies(first, num, plane):
        made = []
        ks = first if num is None else pl.ds(first, num)
        for slot, axis, me, size in ((0, "cols", me_c, ncols), (1, "cols", me_c, ncols),
                                     (2, "rows", me_r, nrows), (3, "rows", me_r, nrows)):
            side = slot % 2
            target = me + 1 if side == 0 else me - 1
            has_target = me < size - 1 if side == 0 else me > 0
            has_source = me > 0 if side == 0 else me < size - 1
            if axis == "cols":
                src, dst = fy.at[ks, 1 - side], hy.at[ks, side]
            else:
                src, dst = plane(1 - side), hx.at[ks, side]
            made.append((has_target, has_source, pltpu.make_async_remote_copy(
                src_ref=src, dst_ref=dst, send_sem=hs_sem.at[first, slot],
                recv_sem=hr_sem.at[first, slot], device_id={axis: target}, device_id_type=MESH)))
        return made

    sent = []

    def send(copies):
        sent.extend(copies)
        for has_target, _, copy in copies:
            @pl.when(has_target)
            def _(copy=copy):
                copy.start()

    def arrive(copies):
        for _, has_source, copy in copies:
            @pl.when(has_source)
            def _(copy=copy):
                copy.wait_recv()

    def plane_start(side):
        return 0 if side == 0 else count - ny

    for cp in loads[:2 * nh]:
        cp.wait()
    for i in range(2):
        for side in range(2):
            for h in range(nh):
                fy[i, side, h] = ku[i, h, strided(side), :]
    pl.semaphore_wait(barrier, len(greeted))
    first = face_copies(0, 2, lambda side: ku.at[:, :, pl.ds(plane_start(side), ny), :])
    send(first)

    def wide(ref, base, rows):
        return jnp.concatenate([ref[h, pl.ds(base, rows), :] for h in range(nh)], axis=1)

    def put(ref, base, rows, value):
        for h in range(nh):
            ref[h, pl.ds(base, rows), :] = value[:, h * LANES:(h + 1) * LANES]

    lane = lax.broadcasted_iota(jnp.int32, (step_rows, nz), 1)
    row = lax.broadcasted_iota(jnp.int32, (step_rows, nz), 0)
    sixteenth = 0.5 / SCALE
    y_mask = jnp.where(lax.rem(row, ny) == ny - 1, 0.0, sixteenth).astype(F32)
    z_mask = jnp.where(lane == nz - 1, 0.0, sixteenth).astype(F32)
    z_edge = jnp.where((lane == nz - 1) | (lane == 0), sixteenth, 0.0).astype(F32)
    kk, uu = ku.at[0], ku.at[1]

    @pl.loop(0, count // step_rows)
    def _(i):
        base = pl.multiple_of(i * step_rows, step_rows)
        here = wide(kk, base, step_rows)
        put(cx, base, step_rows, (here + wide(kk, base + ny, step_rows)) * sixteenth)
        above = (here + pltpu.roll(here, step_rows - 1, 0)) * y_mask
        put(cy, base, step_rows, above)
        put(cyb, base, step_rows, pltpu.roll(above, 1, 0))
        after = (here + pltpu.roll(here, nz - 1, 1)) * z_mask
        put(cz, base, step_rows, after)
        put(czb, base, step_rows, pltpu.roll(after, 1, 1))
    cx[:, pl.ds(count - ny, ny), :] = zero_plane

    def interior(src, dst, shift, residual):
        def body(i, flux_before):
            base = pl.multiple_of(i * step_rows, step_rows)
            val = wide(src, base, step_rows)
            flux_x = wide(cx, base, step_rows) * (val - wide(src, base + ny, step_rows))
            total = flux_x - jnp.concatenate([flux_before, flux_x[:step_rows - ny]], axis=0)
            total = total + wide(cy, base, step_rows) * (val - pltpu.roll(val, step_rows - 1, 0))
            total = total + wide(cyb, base, step_rows) * (val - pltpu.roll(val, 1, 0))
            total = total + wide(cz, base, step_rows) * (val - pltpu.roll(val, nz - 1, 1))
            total = total + wide(czb, base, step_rows) * (val - pltpu.roll(val, 1, 1))
            total = total + (wide(kk, base, step_rows) * z_edge - shift) * val
            if residual:
                total = wide(rs, base, step_rows) - SCALE * total
            put(dst, base, step_rows, total)
            return flux_x[step_rows - ny:]
        lax.fori_loop(0, count // step_rows, body, jnp.zeros((ny, nz), F32))

    def corrections(k, src, dst, sign, pack):
        for side in range(2):
            at = pl.ds(plane_start(side), ny)
            dst[:, at, :] = dst[:, at, :] + sign * (cfx[side] * (src[:, at, :] - hx[k, side]))
        for side in range(2):
            for h in range(nh):
                new = dst[h, strided(side), :] + sign * (
                    cfy[side, h] * (fy[k, side, h] - hy[k, side, h]))
                dst[h, strided(side), :] = new
                if pack:
                    fy[k + 1, side, h] = new

    for cp in loads[2 * nh:]:
        cp.wait()
    interior(uu, v0, 0.0, True)
    arrive(first)
    for side in range(2):
        at = pl.ds(plane_start(side), ny)
        cfx[side] = (kk[:, at, :] + hx[0, side]) * sixteenth
        cfy[side] = (fy[0, side] + hy[0, side]) * sixteenth
    corrections(1, uu, v0, -SCALE, True)

    sums = {}

    def gram_with(k):
        def body(i, accs):
            base = pl.multiple_of(i * 16, 16)
            accs = list(accs)
            for h in range(nh):
                for sub in range(2):
                    at = pl.ds(base + 8 * sub, 8)
                    mine = vecs[k][h, at, :]
                    for j in range(k + 1):
                        other = mine if j == k else vecs[j][h, at, :]
                        accs[j] = accs[j] + mine * other
            return tuple(accs)
        accs = lax.fori_loop(0, count // 16, body,
                             tuple(jnp.zeros((8, LANES), F32) for _ in range(k + 1)), unroll=2)
        for j in range(k + 1):
            sums[j, k] = accs[j]

    outs = []

    def write_out(k):
        for h in range(nh):
            outs.append(pltpu.make_async_copy(
                (vecs[k] if k < 5 else uu).at[h, pl.ds(0, count), :], v_out.at[k, :, pl.ds(h * LANES, LANES)],
                out_sem.at[k, h]))
            outs[-1].start()

    write_out(5)
    for k in range(4):
        vec = vecs[k]
        copies = face_copies(2 + k, None,
                             lambda side, vec=vec: vec.at[:, pl.ds(plane_start(side), ny), :])
        send(copies)
        write_out(k)
        interior(vec, vecs[k + 1], SHIFTS[k] / SCALE, False)
        gram_with(k)
        arrive(copies)
        corrections(2 + k, vec, vecs[k + 1], 1.0, k < 3)
    write_out(4)
    gram_with(4)

    def exchange(p, buf, ssem, rsem, peers, slot, value):
        buf[p, slot(0, 0)] = value
        for e, (dr, dc) in enumerate(peers):
            copy = pltpu.make_async_remote_copy(
                src_ref=buf.at[p, slot(0, 0)], dst_ref=buf.at[p, slot(0, 0)],
                send_sem=ssem.at[p, e], recv_sem=rsem.at[p, e],
                device_id=(lax.rem(me_r + dr, nrows), lax.rem(me_c + dc, ncols)),
                device_id_type=MESH)
            copy.start()
            sent.append((None, None, copy))
        for e, (dr, dc) in enumerate(peers):
            pltpu.make_async_remote_copy(
                src_ref=buf.at[p, slot(0, 0)], dst_ref=buf.at[p, slot(nrows - dr, ncols - dc)],
                send_sem=ssem.at[p, e], recv_sem=rsem.at[p, e],
                device_id=(lax.rem(me_r + nrows - dr, nrows), lax.rem(me_c + ncols - dc, ncols)),
                device_id_type=MESH).wait_recv()
        parts = [buf[p, i] for i in range(len(peers) + 1)]
        while len(parts) > 1:
            parts = [a + b for a, b in zip(parts[::2], parts[1::2])] + (
                parts[-1:] if len(parts) % 2 else [])
        return parts[0]

    def col_of(dc):
        return lax.rem(me_c + dc, ncols)

    def row_of(dr):
        return lax.rem(me_r + dr, nrows)

    pair_row = lax.broadcasted_iota(jnp.int32, (16, LANES), 0)
    on_diag = pair_row == lax.broadcasted_iota(jnp.int32, (16, LANES), 1)

    def all_reduce(p, values):
        for e, pair in enumerate(PAIRS):
            gm[e:e + 1, :] = jnp.sum(values[pair], axis=0, keepdims=True)
        line = jnp.sum(jnp.where(on_diag, jnp.sum(gm[...], axis=1, keepdims=True), 0.0),
                       axis=0, keepdims=True)
        if one_stage:
            line = exchange(p, g1, s1, r1, everyone,
                            lambda dr, dc: row_of(dr) * ncols + col_of(dc), line)
        else:
            line = exchange(p, g1, s1, r1, [(0, d) for d in range(1, ncols)],
                            lambda dr, dc: col_of(dc), line)
            line = exchange(p, g2, s2, r2, [(d, 0) for d in range(1, nrows)],
                            lambda dr, dc: row_of(dr), line)
        gm[...] = jnp.broadcast_to(
            jnp.sum(jnp.where(on_diag, line, 0.0), axis=1, keepdims=True), gm.shape)
        full = {pair: gm[e:e + 1, :] for e, pair in enumerate(PAIRS)}
        return lambda i, j: full[j, i]

    gm[...] = jnp.zeros(gm.shape, F32)
    low_one, inv_one = cholesky(all_reduce(0, sums), 5)
    linv_one = lower_inverse(low_one, inv_one, 5)
    splat = {key: jnp.broadcast_to(val, (8, LANES)) for key, val in linv_one.items()}

    def body(i, accs):
        base = pl.multiple_of(i * 16, 16)
        accs = list(accs)
        for h in range(nh):
            for sub in range(2):
                at = pl.ds(base + 8 * sub, 8)
                raw = [vec[h, at, :] for vec in vecs]
                ortho = []
                for r in range(5):
                    val = splat[r, 0] * raw[0]
                    for c in range(1, r + 1):
                        val = val + splat[r, c] * raw[c]
                    ortho.append(val)
                for e, (a, b) in enumerate(PAIRS):
                    accs[e] = accs[e] + ortho[a] * ortho[b]
        return tuple(accs)
    accs = lax.fori_loop(0, count // 16, body, tuple(jnp.zeros((8, LANES), F32) for _ in PAIRS), unroll=2)

    low_two, inv_two = cholesky(all_reduce(1, dict(zip(PAIRS, accs))), 5)
    linv_two = lower_inverse(low_two, inv_two, 5)

    def add_up(terms):
        return functools.reduce(lambda a, b: a + b, terms)

    trans = {(i, j): add_up([linv_two[i, m] * linv_one[m, j] for m in range(j, i + 1)])
             for i in range(5) for j in range(i + 1)}
    rfac = {(i, j): add_up([low_two[m, i] * low_one[j, m] for m in range(i, j + 1)])
            for i in range(5) for j in range(i, 5)}
    shifted = {}
    for k in range(4):
        for i in range(k + 2):
            val = rfac[i, k + 1] * SCALE
            shifted[i, k] = val + rfac[i, k] * SHIFTS[k] if i <= k else val
    hess = {(i, k): add_up([shifted[i, m] * trans[k, m] for m in range(max(i - 1, 0), k + 1)])
            for k in range(4) for i in range(k + 2)}
    target, inv_n = [rfac[0, 0]], []
    for k in range(4):
        top, bottom = hess[k, k], hess[k + 1, k]
        square = top * top + bottom * bottom
        inv_n.append(inv_sqrt(square))
        cosine, sine = top * inv_n[k], bottom * inv_n[k]
        for j in range(k + 1, 4):
            upper, under = hess[k, j], hess[k + 1, j]
            hess[k, j] = cosine * upper + sine * under
            hess[k + 1, j] = cosine * under - sine * upper
        target.append(-(sine * target[k]))
        target[k] = cosine * target[k]
    weights = [None] * 4
    for i in range(3, -1, -1):
        val = target[i]
        for m in range(i + 1, 4):
            val = val - hess[i, m] * weights[m]
        weights[i] = val * inv_n[i]

    root = math.sqrt(nrows * ncols * nx * ny * nz)
    for e, (j, i) in enumerate(PAIRS):
        coef_out[e:e + 1, :] = trans[i, j] * root
    for k in range(4):
        coef_out[16 + k:17 + k, :] = weights[k] * (1.0 / root)
    one_row = lax.broadcasted_iota(jnp.int32, (1, LANES), 1)
    for i in range(5):
        line = jnp.zeros((1, LANES), F32)
        for j in range(i, 5):
            line = jnp.where(one_row == j, rfac[i, j], line)
        coef_out[24 + i:25 + i, :] = line

    for cp in outs:
        cp.wait()
    for has_target, _, copy in sent:
        if has_target is None:
            copy.wait_send()
        else:
            @pl.when(has_target)
            def _(copy=copy):
                copy.wait_send()


def finish_kernel(v_ref, coef_ref, basis_ref, rfac_ref, updated_ref):
    _, rows, nz = v_ref.shape
    trans = {(i, j): jnp.broadcast_to(coef_ref[e:e + 1, :], (8, LANES))
             for e, (j, i) in enumerate(PAIRS)}
    weights = [jnp.broadcast_to(coef_ref[16 + k:17 + k, :], (8, LANES)) for k in range(4)]

    def body(n, carry):
        at = pl.ds(pl.multiple_of(n * 8, 8), 8)
        for h in range(nz // LANES):
            lanes = pl.ds(h * LANES, LANES)
            raw = [v_ref[k, at, lanes] for k in range(5)]
            new = v_ref[5, at, lanes]
            for i in range(5):
                val = trans[i, 0] * raw[0]
                for j in range(1, i + 1):
                    val = val + trans[i, j] * raw[j]
                basis_ref[i, at, lanes] = val
                if i < 4:
                    new = new + weights[i] * val
            updated_ref[at, lanes] = new
        return carry
    lax.fori_loop(0, rows // 8, body, 0, unroll=4)
    rfac_ref[...] = coef_ref[24:29, 0:5]


def on_device(nrows, ncols, right_side, initial, conduct):
    nx, ny, nz = initial.shape
    nh, count = nz // LANES, nx * ny
    flat = [a.reshape(count, nz) for a in (right_side, initial, conduct)]
    dma = pltpu.SemaphoreType.DMA
    slots = nrows * ncols
    vec = pltpu.VMEM((nh, count + ny, LANES), F32)
    plain = pltpu.VMEM((nh, count, LANES), F32)
    vectors, coefs = pl.pallas_call(
        functools.partial(cycle_kernel, (nrows, ncols, nx, ny, nz)),
        out_shape=(pltpu.VMEM((6, count, nz), F32),
                   pltpu.VMEM((32, LANES), F32)),
        in_specs=[pl.BlockSpec(memory_space=pltpu.HBM)] * 3,
        out_specs=(pl.BlockSpec(memory_space=pl.ANY), pl.BlockSpec(memory_space=pltpu.VMEM)),
        scratch_shapes=[
            pltpu.VMEM((2, nh, count + ny, LANES), F32), plain, vec, vec, vec, vec, plain,
            plain, plain, plain, plain, plain,
            pltpu.VMEM((2, nh, ny, LANES), F32), pltpu.VMEM((2, nh, nx, LANES), F32),
            pltpu.VMEM((6, 2, nh, nx, LANES), F32),
            pltpu.VMEM((6, 2, nh, ny, LANES), F32), pltpu.VMEM((6, 2, nh, nx, LANES), F32),
            pltpu.VMEM((2, slots, 1, LANES), F32), pltpu.VMEM((2, nrows, 1, LANES), F32),
            pltpu.VMEM((16, LANES), F32),
            dma((3, nh)), dma((6, nh)), dma((6, 4)), dma((6, 4)),
            dma((2, slots)), dma((2, slots)), dma((2, nrows)), dma((2, nrows)),
        ],
        compiler_params=pltpu.CompilerParams(
            collective_id=0, has_side_effects=True, vmem_limit_bytes=56 << 20),
        name="cycle",
    )(*flat)
    block = 256
    basis, rfactor, updated = pl.pallas_call(
        finish_kernel,
        grid=(count // block,),
        out_shape=(jax.ShapeDtypeStruct((5, count, nz), F32),
                   jax.ShapeDtypeStruct((5, 5), F32),
                   jax.ShapeDtypeStruct((count, nz), F32)),
        in_specs=[pl.BlockSpec((6, block, nz), lambda i: (0, i, 0)),
                  pl.BlockSpec((32, LANES), lambda i: (0, 0))],
        out_specs=(pl.BlockSpec((5, block, nz), lambda i: (0, i, 0)),
                   pl.BlockSpec((5, 5), lambda i: (0, 0)),
                   pl.BlockSpec((block, nz), lambda i: (i, 0))),
        compiler_params=pltpu.CompilerParams(vmem_limit_bytes=20 << 20),
        name="finish",
    )(vectors, coefs)
    return (basis.reshape(5, nx, ny, nz), rfactor, updated.reshape(nx, ny, nz))


def solution(mesh):
    nrows, ncols = mesh.shape["rows"], mesh.shape["cols"]
    return jax.shard_map(
        functools.partial(on_device, nrows, ncols),
        mesh=mesh,
        in_specs=(P("rows", "cols", None),) * 3,
        out_specs=(P(None, "rows", "cols", None), P(), P("rows", "cols", None)),
        check_vma=False,
    )
```
